32 devices in a mesh: row: 16 (over z, y, x), col: 2 (over core).
Axes of the slice: x: 2, y: 2, z: 4, core: 2. Of those that a mesh axis runs over, the one named last changes fastest.
Arguments:
- matrix: float32 [2, 16, 4, 2, 256, 256], P(None, 'row', None, 'col'), as said below
- keep_mask: int32 [2, 16, 4, 2], P(None, 'row', None, 'col'), may hold values 0 or 1
Outputs:
- factored: float32 [2, 16, 4, 2, 256, 256], P(None, 'row', None, 'col')
The draws below stay inside these ranges and needn't reach their ends.
Inputs may be any that keep to these rules, and one draw needn't show every extreme that they name: `matrix`: tiles whose row and column index are equal are symmetric, and the symmetric completion of the kept tiles in the window's leading two tile rows and columns is positive definite, so that both panel steps meet positive definite diagonal tiles.
All inputs are finite; a program needn't handle non-finite values. No bound on the sum of `keep_mask` on one device may be relied on, other than what follows from the above.
Results may differ from the reference program's by a relative error of at most 0.0001.
Values sent between devices are 32-bit elements; how exact they have to be, the bound alone decides.
No kernel may reach another device: no remote copies, remote signals or barrier semaphores. Data moves between devices by JAX's collectives and lax.ppermute only.
A program may use at most 64 MiB of HBM per device.

```python
import math
import jax
import jax.numpy as jnp
from jax import lax

B = 256
HALF_BAND = 256
TR = 2
CP = 4
TILE_ROWS = 32
TILE_COLS = 8
N_ROW = 16


def wendland_tile(tile_edge):
    positions = jnp.arange(tile_edge, dtype=jnp.float32)
    distance = jnp.abs(positions[:, None] - positions[None, :]) / 16.0
    remain = jnp.maximum(1.0 - distance, 0.0)
    return remain * remain * remain * (3.0 * distance + 1.0)


def draw_matrix(key, part):
    full_shape = (TR, N_ROW, CP, 2, B, B)
    key_entries, key_lift = jax.random.split(jax.random.fold_in(key, 17), 2)
    noise_draw = jax.random.uniform(key_entries, full_shape, jnp.float32, -0.5, 0.5)
    tile_row = (jnp.arange(TR)[:, None] * N_ROW + jnp.arange(N_ROW)[None, :]).reshape(TR, N_ROW, 1, 1, 1, 1)
    tile_col = (2 * jnp.arange(CP)[:, None] + jnp.arange(2)[None, :]).reshape(1, 1, CP, 2, 1, 1)
    on_diag = tile_row == tile_col
    mirrored = 0.5 * (noise_draw + jnp.swapaxes(noise_draw, -1, -2))
    lift_draw = jax.random.uniform(key_lift, (TR, N_ROW, CP, 2, B), jnp.float32, 1.5, 2.5)
    identity = jnp.eye(B, dtype=jnp.float32)
    diagonal = 0.5 * math.sqrt(2.0 * B) * lift_draw[..., None] * identity
    kernel_part = 6.0 * wendland_tile(B)
    values = jnp.where(on_diag, mirrored + diagonal + kernel_part, noise_draw)
    return values


def set_ends(result, rng, least, largest):
    dims = result.shape
    index_at = [jax.random.randint(jax.random.fold_in(rng, axis), (), 0, dims[axis]) for axis in range(len(dims))]
    result = result.at[tuple(index_at)].set(least)
    longest = dims.index(max(dims))
    index_at[longest] = (index_at[longest] + 1) % dims[longest]
    return result.at[tuple(index_at)].set(largest)


def setup_inputs(seed: int = 0) -> dict:
    key_list = jax.random.split(jax.random.key(seed), 3)
    return {
        "matrix": draw_matrix(jax.random.fold_in(key_list[2], 71), 0),
        "keep_mask": set_ends((jax.random.randint(key_list[1], (TR, N_ROW, CP, 2), 0, 4) < 3).astype(jnp.int32), jax.random.fold_in(key_list[1], 1), 0, 1),
    }


def right_solve(factor_diag, blocks):
    block_count, tile_edge = (blocks.shape[0], blocks.shape[1])
    stacked = jnp.transpose(blocks, (2, 0, 1)).reshape(tile_edge, block_count * tile_edge)
    solved = lax.linalg.triangular_solve(factor_diag, stacked, left_side=True, lower=True)
    return jnp.transpose(solved.reshape(tile_edge, block_count, tile_edge), (1, 2, 0))

def reference(matrix, keep_mask):
    blocks = matrix.reshape(TILE_ROWS, TILE_COLS, B, B)
    kept_marks = keep_mask.reshape(TILE_ROWS, TILE_COLS)
    tile_row = jnp.arange(TILE_ROWS, dtype=jnp.int32)[:, None]
    tile_col = jnp.arange(TILE_COLS, dtype=jnp.int32)[None, :]
    kept_tile = ((kept_marks == 1) | (tile_row == tile_col)) & (tile_row >= tile_col) & (tile_row - tile_col <= HALF_BAND)
    blocks = jnp.where(kept_tile[:, :, None, None], blocks, 0.0)
    lower_part = tile_row >= tile_col
    row_index = tile_row[:, :, None]
    for panel_step in range(2):
        factor_diag = jnp.linalg.cholesky(blocks[panel_step, panel_step])
        solved = right_solve(factor_diag, blocks[:, panel_step])
        panel_col = jnp.where(row_index > panel_step, solved, jnp.where(row_index == panel_step, factor_diag[None], 0.0))
        blocks = blocks.at[:, panel_step].set(panel_col)
        column_set = panel_col[:TILE_COLS]
        selected = lower_part & (tile_col > panel_step)

        def update_row(inputs):
            row_blocks, row_panel, row_selected = inputs
            product = jnp.einsum('ab,scb->sac', row_panel.astype(jnp.float32), column_set.astype(jnp.float32), precision=lax.Precision.HIGHEST, preferred_element_type=jnp.float32)
            return row_blocks - jnp.where(row_selected[:, None, None], product, 0.0)
        blocks = lax.map(update_row, (blocks, panel_col, selected))
    return blocks.reshape(TR, N_ROW, CP, 2, B, B)
```

```python
import jax
import jax.numpy as jnp
from jax import lax
from jax.experimental import pallas as pl
from jax.experimental.pallas import tpu as pltpu
from jax.sharding import PartitionSpec as P

HALF_BAND = 256
F32 = jnp.float32
VMEM = pl.BlockSpec(memory_space=pltpu.VMEM)
SMEM = pl.BlockSpec(memory_space=pltpu.SMEM)


def dot(a, b, da, db):
    return lax.dot_general(
        a,
        b,
        (((da,), (db,)), ((), ())),
        precision=lax.Precision.HIGHEST,
        preferred_element_type=F32,
    )


def lanes(x, j):
    return jnp.broadcast_to(x[:, j : j + 1], x.shape)


def rows(x, r):
    return jnp.broadcast_to(x[r : r + 1, :], x.shape)


def factor128(a):
    n = a.shape[0] // 8
    sub = lax.broadcasted_iota(jnp.int32, (8, 128), 0)
    lane = lax.broadcasted_iota(jnp.int32, (8, 128), 1)
    left = [a[8 * i : 8 * i + 8, :] for i in range(n)]
    right = [jnp.where(lane == sub + 8 * i, 1.0, 0.0).astype(F32) for i in range(n)]
    upper, inverse = [], []
    for k in range(n):
        column = [lanes(left[k], 8 * k + s) for s in range(8)]
        pivot = {(r, s): rows(column[s], r) for s in range(8) for r in range(s, 8)}
        low, scale = {}, []
        for s in range(8):
            scale.append(lax.rsqrt(pivot[s, s]))
            for r in range(s + 1, 8):
                low[r, s] = pivot[r, s] * scale[s]
            for t in range(s + 1, 8):
                for r in range(t, 8):
                    pivot[r, t] = pivot[r, t] - low[r, s] * low[t, s]
        u, v = [], []
        for s in range(8):
            x, y = rows(left[k], s), rows(right[k], s)
            for t in range(s):
                x, y = x - low[s, t] * u[t], y - low[s, t] * v[t]
            u.append(x * scale[s])
            v.append(y * scale[s])
        x, y = u[7], v[7]
        for s in range(6, -1, -1):
            x, y = jnp.where(sub == s, u[s], x), jnp.where(sub == s, v[s], y)
        upper.append(x)
        inverse.append(y)
        if k + 1 < n:
            solved = []
            for s in range(8):
                x = lanes(left[k + 1], 8 * k + s)
                for t in range(s):
                    x = x - low[s, t] * solved[t]
                solved.append(x * scale[s])
            for s in range(8):
                left[k + 1] = left[k + 1] - solved[s] * u[s]
                right[k + 1] = right[k + 1] - solved[s] * v[s]
        if k + 2 < n:
            for s in range(7, -1, -1):
                for t in range(s + 1, 8):
                    u[s], v[s] = u[s] - low[t, s] * u[t], v[s] - low[t, s] * v[t]
                u[s], v[s] = u[s] * scale[s], v[s] * scale[s]
            for i in range(k + 2, n):
                column = [lanes(left[i], 8 * k + s) for s in range(8)]
                for s in range(8):
                    left[i] = left[i] - column[s] * u[s]
                    right[i] = right[i] - column[s] * v[s]
    return jnp.concatenate(upper, 0), jnp.concatenate(inverse, 0)


def inverse_factor(a_ref, out_ref):
    h = a_ref.shape[0] // 2
    _, inv0 = factor128(a_ref[:h, :h])
    upper = dot(inv0, a_ref[:h, h:], 1, 0)
    _, inv1 = factor128(a_ref[h:, h:] - dot(upper, upper, 0, 0))
    out_ref[:h, :h] = inv0
    out_ref[:h, h:] = jnp.zeros((h, h), F32)
    out_ref[h:, :h] = -dot(inv1, dot(upper, inv0, 0, 0), 1, 0)
    out_ref[h:, h:] = inv1


def first_kernel(place_ref, own_ref, other_ref, inv_ref, tile_ref):
    tile_ref[...] = jnp.where(place_ref[1] == 0, own_ref[...], other_ref[...])
    inverse_factor(tile_ref, inv_ref)


def second_kernel(place_ref, own_ref, other_ref, inv0_ref, low_ref, inv1_ref, tile_ref):
    first = place_ref[1] == 0
    below = jnp.where(first, own_ref[...], other_ref[...])
    low = dot(below, inv0_ref[...], 1, 1)
    low_ref[...] = low
    tile_ref[...] = jnp.where(first, other_ref[...], own_ref[...]) - dot(low, low, 1, 1)
    inverse_factor(tile_ref, inv1_ref)


def solve(left, right, inv0, low, inv1):
    first = dot(left, inv0, 1, 1)
    return first, dot(right - dot(first, low, 1, 1), inv1, 1, 1)


def last_kernel(
    place_ref, keep_ref, tiles_ref, own_ref, other_ref, near_ref, far_ref,
    inv0_ref, low_ref, inv1_ref, out_ref, panel_ref,
):
    p, q = place_ref[0], place_ref[1]
    row_devices = place_ref[2]
    edge = tiles_ref.shape[-1]
    inv0, low, inv1 = inv0_ref[...], low_ref[...], inv1_ref[...]
    lower = lax.broadcasted_iota(jnp.int32, (edge, edge), 0) >= lax.broadcasted_iota(
        jnp.int32, (edge, edge), 1
    )
    pairs = tiles_ref.shape[1]
    base = lax.rem(p, 8) // 2
    for s in range(1, pairs):
        slot = jnp.bitwise_xor(base, s)
        slot = jnp.where(q == 0, slot, (slot % 2) * 2 + slot // 2)
        source = slot % 2
        left = jnp.where(slot < 2, near_ref[source, 0], far_ref[source, 0])
        right = jnp.where(slot < 2, near_ref[source, 1], far_ref[source, 1])
        panel_ref[s, 0], panel_ref[s, 1] = solve(left, right, inv0, low, inv1)
    for t in range(tiles_ref.shape[0]):
        i = t * row_devices + p
        left = jnp.where(q == 0, own_ref[t], other_ref[t])
        right = jnp.where(q == 0, other_ref[t], own_ref[t])
        first, second = solve(left, right, inv0, low, inv1)
        first = jnp.where((i > 0) | lower, first, 0.0)
        second = jnp.where((i > 1) | ((i == 1) & lower), second, 0.0)
        out_ref[t, 0] = jnp.where(q == 0, first, second)
        for s in range(1, pairs):
            tile = jnp.where(keep_ref[t, s] == 1, tiles_ref[t, s], 0.0)
            out_ref[t, s] = tile

            @pl.when(2 * s + q <= i)
            def _():
                out_ref[t, s] = tile - (
                    dot(first, panel_ref[s, 0], 1, 1) + dot(second, panel_ref[s, 1], 1, 1)
                )


def call(kernel, name, outs, specs, scratch, flops, *args):
    return pl.pallas_call(
        kernel,
        out_shape=outs,
        in_specs=specs,
        out_specs=jax.tree.map(lambda _: VMEM, outs),
        scratch_shapes=scratch,
        name=name,
        cost_estimate=pl.CostEstimate(flops=flops, bytes_accessed=1 << 20, transcendentals=0),
        compiler_params=pltpu.CompilerParams(vmem_limit_bytes=48 << 20),
    )(*args)


def local(matrix, keep_mask):
    tiles = matrix[:, 0, :, 0]
    row_count, pair_count, edge = tiles.shape[0], tiles.shape[1], tiles.shape[-1]
    n = lax.axis_size("row")
    p, q = lax.axis_index("row"), lax.axis_index("col")
    tile_row = jnp.arange(row_count, dtype=jnp.int32)[:, None] * n + p
    tile_col = 2 * jnp.arange(pair_count, dtype=jnp.int32)[None, :] + q
    keep = (
        ((keep_mask[:, 0, :, 0] == 1) | (tile_row == tile_col))
        & (tile_row >= tile_col)
        & (tile_row - tile_col <= HALF_BAND)
    ).astype(jnp.int32)
    place = jnp.stack([p, q, jnp.int32(n)]).astype(jnp.int32)

    def send(x, pairs):
        return lax.ppermute(x, ("row", "col"), [(2 * a + b, 2 * c + d) for a, b, c, d in pairs])

    own = jnp.where((keep[:, 0] == 1)[:, None, None], tiles[:, 0], 0.0)
    other = send(own, [(i, c, i, 1 - c) for i in range(n) for c in range(2)])
    mine = own[0]

    bits = [1, 2]
    high = n // 2
    while high > 2:
        bits.append(high)
        high //= 2
    lead, next_lead = mine, mine
    r = send(next_lead, [(1, c, 0, c) for c in range(2)])
    next_lead = jnp.where(p == 0, r, next_lead)
    have = [0]
    for bit in bits:
        r = send(lead, [(i, 0, i + bit, 0) for i in have])
        lead = jnp.where(jnp.bitwise_and(p, bit) > 0, r, lead)
        if bit > 1:
            r = send(next_lead, [(i, c, i + bit, c) for i in have for c in range(2)])
            next_lead = jnp.where(jnp.bitwise_and(p, bit) > 0, r, next_lead)
        have = have + [i + bit for i in have]
    lead_other = send(lead, [(i, 0, i, 1) for i in range(n)])
    next_other = send(next_lead, [(i, c, i, 1 - c) for i in range(n) for c in range(2)])

    pair = jnp.where(q == 0, jnp.stack([mine, other[0]]), jnp.stack([other[0], mine]))
    size = 8
    while size < n:
        r = send(pair, [(i, i % 2, i + size, i % 2) for i in range(size) if i % 8 > 1])
        pair = jnp.where((p >= size) & (p < 2 * size), r, pair)
        size *= 2
    r = send(pair, [(i, i % 2, i ^ 1, i % 2) for i in range(n) if i % 8 > 1])
    pair = jnp.where(jnp.bitwise_and(p, 1) == q, pair, r)
    flips = (2, 4)
    r = send(pair, [(i, c, i ^ flips[c], c) for i in range(n) for c in range(2)])
    near = jnp.stack([pair, r])
    far = send(near, [(i, c, i ^ flips[1 - c], c) for i in range(n) for c in range(2)])

    tile = jax.ShapeDtypeStruct((edge, edge), F32)
    room = [pltpu.VMEM((edge, edge), F32)]
    inv0 = call(
        first_kernel, "first", tile, [SMEM, VMEM, VMEM], room, 10**10, place, lead, lead_other
    )
    low, inv1 = call(
        second_kernel, "second", [tile, tile], [SMEM, VMEM, VMEM, VMEM], room, 10**10,
        place, next_lead, next_other, inv0,
    )
    out = call(
        last_kernel, "last", jax.ShapeDtypeStruct(tiles.shape, F32),
        [SMEM, SMEM] + [VMEM] * 8, [pltpu.VMEM((pair_count, 2, edge, edge), F32)], 10**10,
        place, keep, tiles, own, other, near, far, inv0, low, inv1,
    )
    return out[:, None, :, None]


def solution(mesh):
    return jax.shard_map(
        local,
        mesh=mesh,
        in_specs=(P(None, "row", None, "col", None, None), P(None, "row", None, "col")),
        out_specs=P(None, "row", None, "col", None, None),
        check_vma=False,
    )
```

```python
import jax
import jax.numpy as jnp
from jax import lax
from jax.experimental import pallas as pl
from jax.experimental.pallas import tpu as pltpu
from jax.sharding import PartitionSpec as P

HALF_BAND = 256
F32 = jnp.float32
VMEM = pl.BlockSpec(memory_space=pltpu.VMEM)
SMEM = pl.BlockSpec(memory_space=pltpu.SMEM)


def dot(a, b, da, db):
    return lax.dot_general(
        a,
        b,
        (((da,), (db,)), ((), ())),
        precision=lax.Precision.HIGHEST,
        preferred_element_type=F32,
    )


def lanes(x, j):
    return jnp.broadcast_to(x[:, j : j + 1], x.shape)


def rows(x, r):
    return jnp.broadcast_to(x[r : r + 1, :], x.shape)


def factor128(a):
    n = a.shape[0] // 8
    sub = lax.broadcasted_iota(jnp.int32, (8, 128), 0)
    lane = lax.broadcasted_iota(jnp.int32, (8, 128), 1)
    left = [a[8 * i : 8 * i + 8, :] for i in range(n)]
    right = [jnp.where(lane == sub + 8 * i, 1.0, 0.0).astype(F32) for i in range(n)]
    upper, inverse = [], []
    for k in range(n):
        column = [lanes(left[k], 8 * k + s) for s in range(8)]
        pivot = {(r, s): rows(column[s], r) for s in range(8) for r in range(s, 8)}
        low, scale = {}, []
        for s in range(8):
            scale.append(lax.rsqrt(pivot[s, s]))
            for r in range(s + 1, 8):
                low[r, s] = pivot[r, s] * scale[s]
            for t in range(s + 1, 8):
                for r in range(t, 8):
                    pivot[r, t] = pivot[r, t] - low[r, s] * low[t, s]
        u, v = [], []
        for s in range(8):
            x, y = rows(left[k], s), rows(right[k], s)
            for t in range(s):
                x, y = x - low[s, t] * u[t], y - low[s, t] * v[t]
            u.append(x * scale[s])
            v.append(y * scale[s])
        x, y = u[7], v[7]
        for s in range(6, -1, -1):
            x, y = jnp.where(sub == s, u[s], x), jnp.where(sub == s, v[s], y)
        upper.append(x)
        inverse.append(y)
        if k + 1 < n:
            solved = []
            for s in range(8):
                x = lanes(left[k + 1], 8 * k + s)
                for t in range(s):
                    x = x - low[s, t] * solved[t]
                solved.append(x * scale[s])
            for s in range(8):
                left[k + 1] = left[k + 1] - solved[s] * u[s]
                right[k + 1] = right[k + 1] - solved[s] * v[s]
        if k + 2 < n:
            for s in range(7, -1, -1):
                for t in range(s + 1, 8):
                    u[s], v[s] = u[s] - low[t, s] * u[t], v[s] - low[t, s] * v[t]
                u[s], v[s] = u[s] * scale[s], v[s] * scale[s]
            for i in range(k + 2, n):
                column = [lanes(left[i], 8 * k + s) for s in range(8)]
                for s in range(8):
                    left[i] = left[i] - column[s] * u[s]
                    right[i] = right[i] - column[s] * v[s]
    return jnp.concatenate(upper, 0), jnp.concatenate(inverse, 0)


def inverse_factor(a_ref, out_ref):
    h = a_ref.shape[0] // 2
    _, inv0 = factor128(a_ref[:h, :h])
    upper = dot(inv0, a_ref[:h, h:], 1, 0)
    _, inv1 = factor128(a_ref[h:, h:] - dot(upper, upper, 0, 0))
    out_ref[:h, :h] = inv0
    out_ref[:h, h:] = jnp.zeros((h, h), F32)
    out_ref[h:, :h] = -dot(inv1, dot(upper, inv0, 0, 0), 1, 0)
    out_ref[h:, h:] = inv1


def first_kernel(place_ref, own_ref, other_ref, inv_ref, tile_ref):
    tile_ref[...] = jnp.where(place_ref[1] == 0, own_ref[...], other_ref[...])
    inverse_factor(tile_ref, inv_ref)


def second_kernel(place_ref, own_ref, other_ref, inv0_ref, low_ref, inv1_ref, tile_ref):
    first = place_ref[1] == 0
    below = jnp.where(first, own_ref[...], other_ref[...])
    low = dot(below, inv0_ref[...], 1, 1)
    low_ref[...] = low
    tile_ref[...] = jnp.where(first, other_ref[...], own_ref[...]) - dot(low, low, 1, 1)
    inverse_factor(tile_ref, inv1_ref)


def solve(left, right, inv0, low, inv1):
    first = dot(left, inv0, 1, 1)
    return first, dot(right - dot(first, low, 1, 1), inv1, 1, 1)


def last_kernel(
    place_ref, keep_ref, tiles_ref, own_ref, other_ref, at_ref, a_ref, b_ref, c_ref,
    inv0_ref, low_ref, inv1_ref, out_ref, panel_ref,
):
    p, q = place_ref[0], place_ref[1]
    row_devices = place_ref[2]
    edge = tiles_ref.shape[-1]
    inv0, low, inv1 = inv0_ref[...], low_ref[...], inv1_ref[...]
    lower = lax.broadcasted_iota(jnp.int32, (edge, edge), 0) >= lax.broadcasted_iota(
        jnp.int32, (edge, edge), 1
    )
    pairs = tiles_ref.shape[1]
    base = lax.rem(p, 8) // 2
    for here, ref in enumerate((at_ref, a_ref, b_ref, c_ref)):
        flip = jnp.where(q == 0, here, (here % 2) * 2 + here // 2)
        slot = jnp.bitwise_xor(base, flip)

        @pl.when(slot > 0)
        def _():
            left = jnp.where(q == 0, ref[0], ref[1])
            right = jnp.where(q == 0, ref[1], ref[0])
            panel_ref[slot, 0], panel_ref[slot, 1] = solve(left, right, inv0, low, inv1)

    for t in range(tiles_ref.shape[0]):
        i = t * row_devices + p
        left = jnp.where(q == 0, own_ref[t], other_ref[t])
        right = jnp.where(q == 0, other_ref[t], own_ref[t])
        first, second = solve(left, right, inv0, low, inv1)
        first = jnp.where((i > 0) | lower, first, 0.0)
        second = jnp.where((i > 1) | ((i == 1) & lower), second, 0.0)
        out_ref[t, 0] = jnp.where(q == 0, first, second)
        for s in range(1, pairs):
            tile = jnp.where(keep_ref[t, s] == 1, tiles_ref[t, s], 0.0)
            out_ref[t, s] = tile

            @pl.when(2 * s + q <= i)
            def _():
                out_ref[t, s] = tile - (
                    dot(first, panel_ref[s, 0], 1, 1) + dot(second, panel_ref[s, 1], 1, 1)
                )


def call(kernel, name, outs, specs, scratch, flops, *args):
    return pl.pallas_call(
        kernel,
        out_shape=outs,
        in_specs=specs,
        out_specs=jax.tree.map(lambda _: VMEM, outs),
        scratch_shapes=scratch,
        name=name,
        cost_estimate=pl.CostEstimate(flops=flops, bytes_accessed=1 << 20, transcendentals=0),
        compiler_params=pltpu.CompilerParams(vmem_limit_bytes=48 << 20),
    )(*args)


def local(matrix, keep_mask):
    tiles = matrix[:, 0, :, 0]
    row_count, pair_count, edge = tiles.shape[0], tiles.shape[1], tiles.shape[-1]
    n = lax.axis_size("row")
    p, q = lax.axis_index("row"), lax.axis_index("col")
    tile_row = jnp.arange(row_count, dtype=jnp.int32)[:, None] * n + p
    tile_col = 2 * jnp.arange(pair_count, dtype=jnp.int32)[None, :] + q
    keep = (
        ((keep_mask[:, 0, :, 0] == 1) | (tile_row == tile_col))
        & (tile_row >= tile_col)
        & (tile_row - tile_col <= HALF_BAND)
    ).astype(jnp.int32)
    place = jnp.stack([p, q, jnp.int32(n)]).astype(jnp.int32)

    def send(x, pairs):
        return lax.ppermute(x, ("row", "col"), [(2 * a + b, 2 * c + d) for a, b, c, d in pairs])

    own = jnp.where((keep[:, 0] == 1)[:, None, None], tiles[:, 0], 0.0)
    other = send(own, [(i, c, i, 1 - c) for i in range(n) for c in range(2)])
    mine = own[0]

    high = []
    while 8 << len(high) < n:
        high.append(8 << len(high))
    lead, next_lead = mine, mine
    r = send(next_lead, [(1, c, 0, c) for c in range(2)])
    next_lead = jnp.where(p == 0, r, next_lead)
    have, next_have = [0], [0, 1]
    for bit in high + [1, 2, 4]:
        r = send(lead, [(i, 0, i + bit, 0) for i in have])
        lead = jnp.where(jnp.bitwise_and(p, bit) > 0, r, lead)
        have = have + [i + bit for i in have]
        if bit != 1:
            r = send(next_lead, [(i, c, i + bit, c) for i in next_have for c in range(2)])
            next_lead = jnp.where(jnp.bitwise_and(p, bit) > 0, r, next_lead)
            next_have = next_have + [i + bit for i in next_have]
    lead_other = send(lead, [(i, 0, i, 1) for i in range(n)])
    next_other = send(next_lead, [(i, c, i, 1 - c) for i in range(n) for c in range(2)])

    mine_here = mine
    for size in high:
        r = send(mine_here, [(i, c, i + size, c) for i in range(size) if i % 8 > 1 for c in range(2)])
        mine_here = jnp.where((p >= size) & (p < 2 * size), r, mine_here)
    sources = [i for i in range(n) if i % 8 > 1]
    r1 = send(
        mine_here,
        [(i, i % 2, i ^ 1, i % 2) for i in sources] + [(i, 1 - i % 2, i, i % 2) for i in sources],
    )
    r2 = send(mine_here, [(i, 1 - i % 2, i ^ 1, i % 2) for i in sources])
    home = jnp.bitwise_and(p, 1) == q
    at = jnp.stack([jnp.where(home, mine_here, r1), jnp.where(home, r1, r2)])
    flips = (2, 4)
    ra = send(at, [(i, c, i ^ flips[c], c) for i in range(n) for c in range(2)])
    rb = send(at, [(i, c, i ^ flips[1 - c], c) for i in range(n) for c in range(2)])
    lead, at = lax.optimization_barrier((lead, at))

    tile = jax.ShapeDtypeStruct((edge, edge), F32)
    room = [pltpu.VMEM((edge, edge), F32)]
    inv0 = call(
        first_kernel, "first", tile, [SMEM, VMEM, VMEM], room, 10**10, place, lead, lead_other
    )
    ra, inv0 = lax.optimization_barrier((ra, inv0))
    rc = send(ra, [(i, c, i ^ flips[1 - c], c) for i in range(n) for c in range(2)])
    low, inv1 = call(
        second_kernel, "second", [tile, tile], [SMEM, VMEM, VMEM, VMEM], room, 10**10,
        place, next_lead, next_other, inv0,
    )
    out = call(
        last_kernel, "last", jax.ShapeDtypeStruct(tiles.shape, F32),
        [SMEM, SMEM] + [VMEM] * 10, [pltpu.VMEM((pair_count, 2, edge, edge), F32)], 10**10,
        place, keep, tiles, own, other, at, ra, rb, rc, inv0, low, inv1,
    )
    return out[:, None, :, None]


def solution(mesh):
    return jax.shard_map(
        local,
        mesh=mesh,
        in_specs=(P(None, "row", None, "col", None, None), P(None, "row", None, "col")),
        out_specs=P(None, "row", None, "col", None, None),
        check_vma=False,
    )
```

```python
import jax
import jax.numpy as jnp
from jax import lax
from jax.experimental import pallas as pl
from jax.experimental.pallas import tpu as pltpu
from jax.sharding import PartitionSpec as P

HALF_BAND = 256
F32 = jnp.float32
BF16 = jnp.bfloat16
VMEM = pl.BlockSpec(memory_space=pltpu.VMEM)
ANY = pl.BlockSpec(memory_space=pl.ANY)
SMEM = pl.BlockSpec(memory_space=pltpu.SMEM)
STEPS = 17 * 16 * 8 + 8


def product(a, b):
    return lax.dot_general(a, b, (((1,), (1,)), ((), ())), preferred_element_type=F32)


def thirds(x):
    high = x.astype(BF16)
    rest = x - high.astype(F32)
    middle = rest.astype(BF16)
    return high, middle, (rest - middle.astype(F32)).astype(BF16)


def left6(x):
    h, m, l = thirds(x)
    return jnp.concatenate([h, h, m, h, l, m], 1)


def right6(x):
    h, m, l = thirds(x)
    return jnp.concatenate([h, m, h, l, h, m], 1)


def left3(x):
    h, m, _ = thirds(x)
    return jnp.concatenate([h, h, m], 1)


def right3(x):
    h, m, _ = thirds(x)
    return jnp.concatenate([h, m, h], 1)


def dot(a, b, da, db):
    return lax.dot_general(
        a,
        b,
        (((da,), (db,)), ((), ())),
        precision=lax.Precision.HIGHEST,
        preferred_element_type=F32,
    )


def lanes(x, j):
    return jnp.broadcast_to(x[:, j : j + 1], x.shape)


def inverse128(a, steps_ref):
    n = a.shape[0] // 8
    sub = lax.broadcasted_iota(jnp.int32, (8, 128), 0)
    lane = lax.broadcasted_iota(jnp.int32, (8, 128), 1)
    count = [0]

    def keep(x):
        at = 8 * count[0]
        count[0] += 1
        steps_ref[at : at + 8, :] = x
        return at

    def row(at, r):
        return steps_ref[pl.ds(at + r, 8, stride=0), :]

    part = [a[8 * i : 8 * i + 8, :] for i in range(n)]
    column = [lanes(part[0], c) for c in range(8)]
    inverse = []
    for k in range(n):
        here = (lane >= 8 * k) & (lane < 8 * k + 8)
        kept = [keep(c) for c in column]
        pivot = {(r, s): row(kept[s], r) for s in range(8) for r in range(s, 8)}
        low, scale, solved = {}, [], []
        if k + 1 < n:
            below = [lanes(part[k + 1], 8 * k + s) for s in range(8)]
            column = [lanes(part[k + 1], 8 * k + 8 + c) for c in range(8)]
        for s in range(8):
            reciprocal = 1.0 / pivot[s, s]
            scale.append(lax.rsqrt(pivot[s, s]))
            for r in range(s + 1, 8):
                low[r, s] = pivot[r, s] * scale[s]
            for t in range(s + 1, 8):
                for r in range(t, 8):
                    pivot[r, t] = pivot[r, t] - (pivot[r, s] * pivot[t, s]) * reciprocal
            if k + 1 < n:
                x = below[s]
                for t in range(s):
                    x = x - low[s, t] * solved[t]
                x = x * scale[s]
                solved.append(x)
                at = keep(x)
                for c in range(8):
                    column[c] = column[c] - x * row(at, c)
        at = keep(jnp.where(here, jnp.where(lane == sub + 8 * k, 1.0, 0.0).astype(F32), part[k]))
        u = []
        for s in range(8):
            x = row(at, s)
            for t in range(s):
                x = x - low[s, t] * u[t]
            u.append(x * scale[s])
        x = u[7]
        for s in range(6, -1, -1):
            x = jnp.where(sub == s, u[s], x)
        inverse.append(jnp.where(lane <= sub + 8 * k, x, 0.0))
        if k + 1 < n:
            x = jnp.where(here, 0.0, part[k + 1])
            for s in range(8):
                x = x - solved[s] * u[s]
            part[k + 1] = x
        if k + 2 < n:
            for s in range(7, -1, -1):
                for t in range(s + 1, 8):
                    u[s] = u[s] - low[t, s] * u[t]
                u[s] = u[s] * scale[s]
            for i in range(k + 2, n):
                x = jnp.where(here, 0.0, part[i])
                for s in range(8):
                    x = x - lanes(part[i], 8 * k + s) * u[s]
                part[i] = x
    return jnp.concatenate(inverse, 0)


def inverse_factor(a_ref, out_ref, steps_ref):
    h = a_ref.shape[0] // 2
    inv0 = inverse128(a_ref[:h, :h], steps_ref)
    upper = dot(inv0, a_ref[:h, h:], 1, 0)
    inv1 = inverse128(a_ref[h:, h:] - dot(upper, upper, 0, 0), steps_ref)
    out_ref[:h, :h] = inv0
    out_ref[:h, h:] = jnp.zeros((h, h), F32)
    out_ref[h:, :h] = -dot(inv1, dot(upper, inv0, 0, 0), 1, 0)
    out_ref[h:, h:] = inv1


def first_kernel(place_ref, tile_ref, out_ref, steps_ref):
    root = (place_ref[0] == 0) & (place_ref[1] == 0)

    @pl.when(root)
    def _():
        inverse_factor(tile_ref, out_ref, steps_ref)

    @pl.when(jnp.logical_not(root))
    def _():
        out_ref[...] = tile_ref[...]


def second_kernel(place_ref, own_ref, other_ref, inv0_ref, low_ref, inv1_ref, tile_ref, steps_ref):
    first = place_ref[1] == 0
    inv0 = jnp.where(first, own_ref[0], other_ref[0])
    inv0_ref[...] = inv0
    low = product(left6(jnp.where(first, own_ref[1], other_ref[1])), right6(inv0))
    low_ref[...] = low
    corner = jnp.where(first, other_ref[0], own_ref[0])
    tile_ref[...] = corner - product(left6(low), right6(low))
    inverse_factor(tile_ref, inv1_ref, steps_ref)


def last_kernel(
    place_ref, keep_ref, inv0_ref, low_ref, inv1_ref, own_ref, other_ref, at_ref, a_ref, b_ref, c_ref,
    tiles_ref, out_ref, own, other, hops, tiles, result, sems, hop_sems, out_sems,
):
    p, q = place_ref[0], place_ref[1]
    edge, count, pairs = tiles_ref.shape[-1], tiles_ref.shape[0], tiles_ref.shape[1]
    copy = pltpu.make_async_copy
    loads = [
        copy(own_ref, own, sems.at[0]),
        copy(other_ref, other, sems.at[1]),
        copy(tiles_ref, tiles, sems.at[2]),
    ]
    hop_loads = [
        copy(ref, hops.at[i], hop_sems.at[i]) for i, ref in enumerate((at_ref, a_ref, b_ref, c_ref))
    ]
    for load in loads[:2] + hop_loads + loads[2:]:
        load.start()
    row = lax.broadcasted_iota(jnp.int32, (edge, edge), 0)
    lower = row >= lax.broadcasted_iota(jnp.int32, (edge, edge), 1)
    inv0, low, inv1 = right6(inv0_ref[...]), right6(low_ref[...]), right6(inv1_ref[...])

    def solve(left, right):
        first = product(left6(left), inv0)
        return first, product(left6(right - product(left6(first), low)), inv1)

    for load in loads[:2] + hop_loads:
        load.wait()
    rows, panels = [], []
    for t in range(count):
        i = t * place_ref[2] + p
        first, second = solve(
            jnp.where(q == 0, own[t], other[t]), jnp.where(q == 0, other[t], own[t])
        )
        first = jnp.where((i > 0) | lower, first, 0.0)
        second = jnp.where((i > 1) | ((i == 1) & lower), second, 0.0)
        result[t, 0] = jnp.where(q == 0, first, second)
        rows.append(left3(jnp.concatenate([first, second], 1)))
    for i in range(4):
        first, second = solve(
            jnp.where(q == 0, hops[i, 0], hops[i, 1]), jnp.where(q == 0, hops[i, 1], hops[i, 0])
        )
        panels.append(right3(jnp.concatenate([first, second], 1)))
    loads[2].wait()
    for i in range(4):
        flip = jnp.where(q == 0, i, (i % 2) * 2 + i // 2)
        s = jnp.bitwise_xor(lax.rem(p, 8) // 2, flip)
        room = jnp.where(s > 0, s, pairs)
        for t in range(count):
            wanted = 2 * s + q <= t * place_ref[2] + p
            tile = jnp.where(keep_ref[t, s] == 1, tiles[t, s], 0.0)
            result[t, room] = tile - jnp.where(wanted, product(rows[t], panels[i]), 0.0)

    for t in range(count):
        copy(result.at[t, pl.ds(0, pairs)], out_ref.at[t], out_sems.at[t]).start()
    for t in range(count):
        copy(result.at[t, pl.ds(0, pairs)], out_ref.at[t], out_sems.at[t]).wait()


def call(kernel, name, outs, specs, scratch, flops, *args, out_specs=VMEM):
    return pl.pallas_call(
        kernel,
        out_shape=outs,
        in_specs=specs,
        out_specs=out_specs,
        scratch_shapes=scratch,
        name=name,
        cost_estimate=pl.CostEstimate(flops=flops, bytes_accessed=1 << 20, transcendentals=0),
        compiler_params=pltpu.CompilerParams(vmem_limit_bytes=48 << 20),
    )(*args)


def after(x, *earlier):
    return lax.optimization_barrier((x,) + earlier)[0]


def local(matrix, keep_mask):
    tiles = matrix[:, 0, :, 0]
    row_count, pair_count, edge = tiles.shape[0], tiles.shape[1], tiles.shape[-1]
    n = lax.axis_size("row")
    p, q = lax.axis_index("row"), lax.axis_index("col")
    tile_row = jnp.arange(row_count, dtype=jnp.int32)[:, None] * n + p
    tile_col = 2 * jnp.arange(pair_count, dtype=jnp.int32)[None, :] + q
    keep = (
        ((keep_mask[:, 0, :, 0] == 1) | (tile_row == tile_col))
        & (tile_row >= tile_col)
        & (tile_row - tile_col <= HALF_BAND)
    ).astype(jnp.int32)
    place = jnp.stack([p, q, jnp.int32(n)]).astype(jnp.int32)

    def send(x, pairs):
        return lax.ppermute(x, ("row", "col"), [(2 * a + b, 2 * c + d) for a, b, c, d in pairs])

    mine = jnp.where(keep[0, 0] == 1, matrix[0, 0, 0, 0], 0.0)
    high = []
    while 8 << len(high) < n:
        high.append(8 << len(high))
    sources = [i for i in range(n) if i % 8 > 1]
    flips = (2, 4)

    def chosen(ps):
        return sum([(p == i).astype(jnp.int32) for i in ps]) > 0

    source = [(0, 0), (1, 0), (1, 1)]
    tile = jax.ShapeDtypeStruct((edge, edge), F32)
    room = pltpu.VMEM((STEPS, edge // 2), F32)
    held = call(first_kernel, "first", tile, [SMEM, VMEM], [room], 10**9, place, mine)
    for bit in high[1:]:
        r = send(held, [(i, c, i + bit, c) for i, c in source])
        held = jnp.where(chosen([i + bit for i, _ in source]), r, held)
        source = source + [(i + bit, c) for i, c in source]
    steps = (2, high[0], high[0] + 2)
    received = [send(held, [(i, c, i + bit, c) for i, c in source]) for bit in steps]
    trail = mine
    for size in high:
        r = send(trail, [(i, c, i + size, c) for i in range(2, size) if i % 8 > 1 for c in range(2)])
        trail = jnp.where((p >= size) & (p < 2 * size), r, trail)
    for bit, r in zip(steps, received):
        held = jnp.where(chosen([i + bit for i, _ in source]), r, held)
    source = source + [(i + bit, c) for bit in steps for i, c in source]
    across = send(held, [(i, c, i ^ 1, c) for i, c in source])
    up = send(held, [(i, c, i + 4, c) for i, c in source])
    both = send(held, [(i, c, (i ^ 1) + 4, c) for i, c in source])
    below, even = jnp.bitwise_and(p, 4) == 0, jnp.bitwise_and(p, 1) == 0
    straight, crossed = jnp.where(below, held, up), jnp.where(below, across, both)
    row0 = jnp.where(even, straight, crossed)
    row1 = jnp.where(even, crossed, straight)
    lead = jnp.stack([jnp.where(q == 0, row0, row1), row1])

    r1 = send(
        trail,
        [(i, i % 2, i ^ 1, i % 2) for i in sources] + [(i, 1 - i % 2, i, i % 2) for i in sources],
    )
    r2 = send(trail, [(i, 1 - i % 2, i ^ 1, i % 2) for i in sources])
    lead_other = send(lead, [(i, c, i, 1 - c) for i in range(n) for c in range(2)])
    home = jnp.bitwise_and(p, 1) == q
    at = jnp.stack([jnp.where(home, trail, r1), jnp.where(home, r1, r2)])
    ra = send(at, [(i, c, i ^ flips[c], c) for i in range(n) for c in range(2)])
    rb = send(at, [(i, c, i ^ flips[1 - c], c) for i in range(n) for c in range(2)])

    lead, at = lax.optimization_barrier((lead, at))
    inv0, low, inv1 = call(
        second_kernel, "second", [tile, tile, tile], [SMEM, VMEM, VMEM],
        [pltpu.VMEM((edge, edge), F32), room], 10**10, place, lead, lead_other, out_specs=[VMEM] * 3,
    )
    rc = send(ra, [(i, c, i ^ flips[1 - c], c) for i in range(n) for c in range(2)])
    own = jnp.stack([mine, jnp.where(keep[1, 0] == 1, matrix[1, 0, 0, 0], 0.0)])
    other = send(after(own, inv1), [(i, c, i, 1 - c) for i in range(n) for c in range(2)])
    out = call(
        last_kernel, "last", jax.ShapeDtypeStruct(tiles.shape, F32),
        [SMEM, SMEM, VMEM, VMEM, VMEM] + [ANY] * 7,
        [
            pltpu.VMEM(own.shape, F32),
            pltpu.VMEM(own.shape, F32),
            pltpu.VMEM((4,) + at.shape, F32),
            pltpu.VMEM(tiles.shape, F32),
            pltpu.VMEM((row_count, pair_count + 1, edge, edge), F32),
            pltpu.SemaphoreType.DMA((3,)),
            pltpu.SemaphoreType.DMA((4,)),
            pltpu.SemaphoreType.DMA((row_count,)),
        ],
        10**10, place, keep, inv0, low, inv1, own, other, at, ra, rb, rc, tiles, out_specs=ANY,
    )
    return out[:, None, :, None]


def solution(mesh):
    return jax.shard_map(
        local,
        mesh=mesh,
        in_specs=(P(None, "row", None, "col", None, None), P(None, "row", None, "col")),
        out_specs=P(None, "row", None, "col", None, None),
        check_vma=False,
    )
```

```python
import jax
import jax.numpy as jnp
from jax import lax
from jax.experimental import pallas as pl
from jax.experimental.pallas import tpu as pltpu
from jax.sharding import PartitionSpec as P

HALF_BAND = 256
F32 = jnp.float32
BF16 = jnp.bfloat16
VMEM = pl.BlockSpec(memory_space=pltpu.VMEM)
ANY = pl.BlockSpec(memory_space=pl.ANY)
SMEM = pl.BlockSpec(memory_space=pltpu.SMEM)
STEPS = 17 * 16 * 8 + 8


def product(a, b):
    return lax.dot_general(a, b, (((1,), (1,)), ((), ())), preferred_element_type=F32)


def thirds(x):
    high = x.astype(BF16)
    rest = x - high.astype(F32)
    middle = rest.astype(BF16)
    return high, middle, (rest - middle.astype(F32)).astype(BF16)


def left6(x):
    h, m, l = thirds(x)
    return jnp.concatenate([h, h, m, h, l, m], 1)


def right6(x):
    h, m, l = thirds(x)
    return jnp.concatenate([h, m, h, l, h, m], 1)


def left3(x):
    h, m, _ = thirds(x)
    return jnp.concatenate([h, h, m], 1)


def right3(x):
    h, m, _ = thirds(x)
    return jnp.concatenate([h, m, h], 1)


def dot(a, b, da, db):
    return lax.dot_general(
        a,
        b,
        (((da,), (db,)), ((), ())),
        precision=lax.Precision.HIGHEST,
        preferred_element_type=F32,
    )


def lanes(x, j):
    return jnp.broadcast_to(x[:, j : j + 1], x.shape)


def inverse128(a, steps_ref):
    n = a.shape[0] // 8
    sub = lax.broadcasted_iota(jnp.int32, (8, 128), 0)
    lane = lax.broadcasted_iota(jnp.int32, (8, 128), 1)
    count = [0]

    def keep(x):
        at = 8 * count[0]
        count[0] += 1
        steps_ref[at : at + 8, :] = x
        return at

    def row(at, r):
        return steps_ref[pl.ds(at + r, 8, stride=0), :]

    part = [a[8 * i : 8 * i + 8, :] for i in range(n)]
    column = [lanes(part[0], c) for c in range(8)]
    inverse = []
    for k in range(n):
        here = (lane >= 8 * k) & (lane < 8 * k + 8)
        kept = [keep(c) for c in column]
        pivot = {(r, s): row(kept[s], r) for s in range(8) for r in range(s, 8)}
        low, scale, solved = {}, [], []
        if k + 1 < n:
            below = [lanes(part[k + 1], 8 * k + s) for s in range(8)]
            column = [lanes(part[k + 1], 8 * k + 8 + c) for c in range(8)]
        for s in range(8):
            reciprocal = 1.0 / pivot[s, s]
            scale.append(lax.rsqrt(pivot[s, s]))
            for r in range(s + 1, 8):
                low[r, s] = pivot[r, s] * scale[s]
            for t in range(s + 1, 8):
                for r in range(t, 8):
                    pivot[r, t] = pivot[r, t] - (pivot[r, s] * pivot[t, s]) * reciprocal
            if k + 1 < n:
                x = below[s]
                for t in range(s):
                    x = x - low[s, t] * solved[t]
                x = x * scale[s]
                solved.append(x)
                at = keep(x)
                for c in range(8):
                    column[c] = column[c] - x * row(at, c)
        at = keep(jnp.where(here, jnp.where(lane == sub + 8 * k, 1.0, 0.0).astype(F32), part[k]))
        u = []
        for s in range(8):
            x = row(at, s)
            for t in range(s):
                x = x - low[s, t] * u[t]
            u.append(x * scale[s])
        x = u[7]
        for s in range(6, -1, -1):
            x = jnp.where(sub == s, u[s], x)
        inverse.append(jnp.where(lane <= sub + 8 * k, x, 0.0))
        if k + 1 < n:
            x = jnp.where(here, 0.0, part[k + 1])
            for s in range(8):
                x = x - solved[s] * u[s]
            part[k + 1] = x
        if k + 2 < n:
            for s in range(7, -1, -1):
                for t in range(s + 1, 8):
                    u[s] = u[s] - low[t, s] * u[t]
                u[s] = u[s] * scale[s]
            for i in range(k + 2, n):
                x = jnp.where(here, 0.0, part[i])
                for s in range(8):
                    x = x - lanes(part[i], 8 * k + s) * u[s]
                part[i] = x
    return jnp.concatenate(inverse, 0)


def inverse_factor(a_ref, out_ref, steps_ref):
    h = a_ref.shape[0] // 2
    inv0 = inverse128(a_ref[:h, :h], steps_ref)
    upper = dot(inv0, a_ref[:h, h:], 1, 0)
    inv1 = inverse128(a_ref[h:, h:] - dot(upper, upper, 0, 0), steps_ref)
    out_ref[:h, :h] = inv0
    out_ref[:h, h:] = jnp.zeros((h, h), F32)
    out_ref[h:, :h] = -dot(inv1, dot(upper, inv0, 0, 0), 1, 0)
    out_ref[h:, h:] = inv1


def first_kernel(place_ref, tile_ref, out_ref, steps_ref):
    root = (place_ref[0] == 0) & (place_ref[1] == 0)

    @pl.when(root)
    def _():
        inverse_factor(tile_ref, out_ref, steps_ref)

    @pl.when(jnp.logical_not(root))
    def _():
        out_ref[...] = tile_ref[...]


def solve(left, right, inv0, low, inv1):
    first = product(left6(left), inv0)
    return first, product(left6(right - product(left6(first), low)), inv1)


def second_kernel(place_ref, own_ref, other_ref, inv0_ref, low_ref, inv1_ref, tile_ref, steps_ref):
    first = place_ref[1] == 0
    inv0 = jnp.where(first, own_ref[0], other_ref[0])
    inv0_ref[...] = inv0
    low = product(left6(jnp.where(first, own_ref[1], other_ref[1])), right6(inv0))
    low_ref[...] = low
    corner = jnp.where(first, other_ref[0], own_ref[0])
    tile_ref[...] = corner - product(left6(low), right6(low))
    inverse_factor(tile_ref, inv1_ref, steps_ref)


def slot_of(place_ref, hop):
    flip = jnp.where(place_ref[1] == 0, hop, (hop % 2) * 2 + hop // 2)
    return jnp.bitwise_xor(lax.rem(place_ref[0], 8) // 2, flip)


def update(place_ref, keep_ref, tile, rows, panel, t, s):
    wanted = 2 * s + place_ref[1] <= t * place_ref[2] + place_ref[0]
    kept = jnp.where(keep_ref[t, s] == 1, tile, 0.0)
    return kept - jnp.where(wanted, product(rows, panel), 0.0)


def third_kernel(
    place_ref, keep_ref, inv0_ref, low_ref, inv1_ref, own_ref, other_ref, at_ref, a_ref, b_ref, tiles_ref,
    out_ref, rows_ref, hops, tiles, result, sems, hop_sems, out_sems,
):
    core0 = place_ref[1] == 0
    edge, count = tiles_ref.shape[-1], tiles_ref.shape[0]
    copy = pltpu.make_async_copy
    loads = [
        copy(ref, hops.at[i], hop_sems.at[i])
        for i, ref in enumerate((own_ref, other_ref, at_ref, a_ref, b_ref))
    ]
    loads.append(copy(tiles_ref, tiles, sems.at[0]))
    for load in loads:
        load.start()
    factors = right6(inv0_ref[...]), right6(low_ref[...]), right6(inv1_ref[...])
    row = lax.broadcasted_iota(jnp.int32, (edge, edge), 0)
    lower = row >= lax.broadcasted_iota(jnp.int32, (edge, edge), 1)
    for load in loads:
        load.wait()
    stores, rows = [], []
    for t in range(count):
        i = t * place_ref[2] + place_ref[0]
        left = jnp.where(core0, hops[0, t], hops[1, t])
        first, second = solve(left, jnp.where(core0, hops[1, t], hops[0, t]), *factors)
        first = jnp.where((i > 0) | lower, first, 0.0)
        second = jnp.where((i > 1) | ((i == 1) & lower), second, 0.0)
        result[t, 3] = jnp.where(core0, first, second)
        rows_ref[t, :, :edge] = first
        rows_ref[t, :, edge:] = second
        rows.append(left3(jnp.concatenate([first, second], 1)))
        stores.append(copy(result.at[t, 3], out_ref.at[t, 0], out_sems.at[t, 3]))
    panels = []
    for i in range(3):
        left = jnp.where(core0, hops[i + 2, 0], hops[i + 2, 1])
        both = solve(left, jnp.where(core0, hops[i + 2, 1], hops[i + 2, 0]), *factors)
        panels.append(right3(jnp.concatenate(both, 1)))
    for i in range(3):
        s = slot_of(place_ref, i)
        for t in range(count):
            result[t, i] = update(place_ref, keep_ref, tiles[t, s], rows[t], panels[i], t, s)
    for store in stores:
        store.start()
    for i in range(3):
        s = slot_of(place_ref, i)

        @pl.when(s > 0)
        def _():
            for t in range(count):
                copy(result.at[t, i], out_ref.at[t, s], out_sems.at[t, i]).start()
            for t in range(count):
                copy(result.at[t, i], out_ref.at[t, s], out_sems.at[t, i]).wait()

    for store in stores:
        store.wait()


def fourth_kernel(
    place_ref, keep_ref, inv0_ref, low_ref, inv1_ref, rows_ref, c_ref, tiles_ref, _,
    out_ref, tiles, result, sems, out_sems,
):
    s = slot_of(place_ref, 3)

    @pl.when(s > 0)
    def _():
        core0 = place_ref[1] == 0
        count = tiles.shape[0]
        copy = pltpu.make_async_copy
        loads = [copy(tiles_ref.at[t, s], tiles.at[t], sems.at[t]) for t in range(count)]
        stores = [copy(result.at[t], out_ref.at[t, s], out_sems.at[t]) for t in range(count)]
        for load in loads:
            load.start()
        factors = right6(inv0_ref[...]), right6(low_ref[...]), right6(inv1_ref[...])
        both = solve(jnp.where(core0, c_ref[0], c_ref[1]), jnp.where(core0, c_ref[1], c_ref[0]), *factors)
        panel = right3(jnp.concatenate(both, 1))
        rows = [left3(rows_ref[t]) for t in range(count)]
        for load in loads:
            load.wait()
        for t in range(count):
            result[t] = update(place_ref, keep_ref, tiles[t], rows[t], panel, t, s)
            stores[t].start()
        for store in stores:
            store.wait()


def call(kernel, name, outs, specs, scratch, flops, *args, out_specs=VMEM, aliases={}):
    return pl.pallas_call(
        kernel,
        out_shape=outs,
        in_specs=specs,
        out_specs=out_specs,
        input_output_aliases=aliases,
        scratch_shapes=scratch,
        name=name,
        cost_estimate=pl.CostEstimate(flops=flops, bytes_accessed=1 << 20, transcendentals=0),
        compiler_params=pltpu.CompilerParams(vmem_limit_bytes=48 << 20),
    )(*args)


def after(x, *earlier):
    return lax.optimization_barrier((x,) + earlier)[0]


def local(matrix, keep_mask):
    tiles = matrix[:, 0, :, 0]
    row_count, pair_count, edge = tiles.shape[0], tiles.shape[1], tiles.shape[-1]
    n = lax.axis_size("row")
    p, q = lax.axis_index("row"), lax.axis_index("col")
    tile_row = jnp.arange(row_count, dtype=jnp.int32)[:, None] * n + p
    tile_col = 2 * jnp.arange(pair_count, dtype=jnp.int32)[None, :] + q
    keep = (
        ((keep_mask[:, 0, :, 0] == 1) | (tile_row == tile_col))
        & (tile_row >= tile_col)
        & (tile_row - tile_col <= HALF_BAND)
    ).astype(jnp.int32)
    place = jnp.stack([p, q, jnp.int32(n)]).astype(jnp.int32)

    def send(x, pairs):
        return lax.ppermute(x, ("row", "col"), [(2 * a + b, 2 * c + d) for a, b, c, d in pairs])

    mine = jnp.where(keep[0, 0] == 1, matrix[0, 0, 0, 0], 0.0)
    high = []
    while 8 << len(high) < n:
        high.append(8 << len(high))
    sources = [i for i in range(n) if i % 8 > 1]
    flips = (2, 4)

    def chosen(ps):
        return sum([(p == i).astype(jnp.int32) for i in ps]) > 0

    source = [(0, 0), (1, 0), (1, 1)]
    tile = jax.ShapeDtypeStruct((edge, edge), F32)
    room = pltpu.VMEM((STEPS, edge // 2), F32)
    held = call(first_kernel, "first", tile, [SMEM, VMEM], [room], 10**9, place, mine)
    for bit in high[1:]:
        r = send(held, [(i, c, i + bit, c) for i, c in source])
        held = jnp.where(chosen([i + bit for i, _ in source]), r, held)
        source = source + [(i + bit, c) for i, c in source]
    steps = (2, high[0], high[0] + 2)
    received = [send(held, [(i, c, i + bit, c) for i, c in source]) for bit in steps]
    trail = mine
    for size in high:
        r = send(trail, [(i, c, i + size, c) for i in range(2, size) if i % 8 > 1 for c in range(2)])
        trail = jnp.where((p >= size) & (p < 2 * size), r, trail)
    for bit, r in zip(steps, received):
        held = jnp.where(chosen([i + bit for i, _ in source]), r, held)
    source = source + [(i + bit, c) for bit in steps for i, c in source]
    across = send(held, [(i, c, i ^ 1, c) for i, c in source])
    up = send(held, [(i, c, i + 4, c) for i, c in source])
    both = send(held, [(i, c, (i ^ 1) + 4, c) for i, c in source])
    below, even = jnp.bitwise_and(p, 4) == 0, jnp.bitwise_and(p, 1) == 0
    straight, crossed = jnp.where(below, held, up), jnp.where(below, across, both)
    row0 = jnp.where(even, straight, crossed)
    row1 = jnp.where(even, crossed, straight)
    lead = jnp.stack([jnp.where(q == 0, row0, row1), row1])

    r1 = send(
        trail,
        [(i, i % 2, i ^ 1, i % 2) for i in sources] + [(i, 1 - i % 2, i, i % 2) for i in sources],
    )
    r2 = send(trail, [(i, 1 - i % 2, i ^ 1, i % 2) for i in sources])
    lead_other = send(lead, [(i, c, i, 1 - c) for i in range(n) for c in range(2)])
    home = jnp.bitwise_and(p, 1) == q
    at = jnp.stack([jnp.where(home, trail, r1), jnp.where(home, r1, r2)])
    ra = send(at, [(i, c, i ^ flips[c], c) for i in range(n) for c in range(2)])
    rb = send(at, [(i, c, i ^ flips[1 - c], c) for i in range(n) for c in range(2)])

    lead, at = lax.optimization_barrier((lead, at))
    inv0, low, inv1 = call(
        second_kernel, "second", [tile, tile, tile], [SMEM, VMEM, VMEM],
        [pltpu.VMEM((edge, edge), F32), room], 10**10, place, lead, lead_other, out_specs=[VMEM] * 3,
    )
    rc = send(ra, [(i, c, i ^ flips[1 - c], c) for i in range(n) for c in range(2)])
    own = jnp.stack([mine, jnp.where(keep[1, 0] == 1, matrix[1, 0, 0, 0], 0.0)])
    other = send(after(own, inv1), [(i, c, i, 1 - c) for i in range(n) for c in range(2)])
    three, five = pltpu.SemaphoreType.DMA((3,)), pltpu.SemaphoreType.DMA((5,))
    out, rows = call(
        third_kernel, "third",
        [
            jax.ShapeDtypeStruct(tiles.shape, F32),
            jax.ShapeDtypeStruct((row_count, edge, 2 * edge), F32),
        ],
        [SMEM, SMEM] + [VMEM] * 3 + [ANY] * 6,
        [
            pltpu.VMEM((5,) + at.shape, F32),
            pltpu.VMEM(tiles.shape, F32),
            pltpu.VMEM((row_count, 4, edge, edge), F32),
            three,
            five,
            pltpu.SemaphoreType.DMA((row_count, 4)),
        ],
        10**10, place, keep, inv0, low, inv1, own, other, at, ra, rb, tiles, out_specs=[ANY, VMEM],
    )
    out = call(
        fourth_kernel, "fourth", jax.ShapeDtypeStruct(tiles.shape, F32),
        [SMEM, SMEM] + [VMEM] * 5 + [ANY] * 2,
        [pltpu.VMEM(own.shape, F32), pltpu.VMEM(own.shape, F32), three, three],
        10**10, place, keep, inv0, low, inv1, rows, rc, tiles, out, out_specs=ANY, aliases={8: 0},
    )
    return out[:, None, :, None]


def solution(mesh):
    return jax.shard_map(
        local,
        mesh=mesh,
        in_specs=(P(None, "row", None, "col", None, None), P(None, "row", None, "col")),
        out_specs=P(None, "row", None, "col", None, None),
        check_vma=False,
    )
```

```python
import jax
import jax.numpy as jnp
from jax import lax
from jax.experimental import pallas as pl
from jax.experimental.pallas import tpu as pltpu
from jax.sharding import PartitionSpec as P

HALF_BAND = 256
F32 = jnp.float32
BF16 = jnp.bfloat16
VMEM = pl.BlockSpec(memory_space=pltpu.VMEM)
ANY = pl.BlockSpec(memory_space=pl.ANY)
SMEM = pl.BlockSpec(memory_space=pltpu.SMEM)
STEPS = 17 * 16 * 8 + 8


def product(a, b):
    return lax.dot_general(a, b, (((1,), (1,)), ((), ())), preferred_element_type=F32)


def thirds(x):
    high = x.astype(BF16)
    rest = x - high.astype(F32)
    middle = rest.astype(BF16)
    return high, middle, (rest - middle.astype(F32)).astype(BF16)


def left6(x):
    h, m, l = thirds(x)
    return jnp.concatenate([h, h, m, h, l, m], 1)


def right6(x):
    h, m, l = thirds(x)
    return jnp.concatenate([h, m, h, l, h, m], 1)


def left3(x):
    h, m, _ = thirds(x)
    return jnp.concatenate([h, h, m], 1)


def right3(x):
    h, m, _ = thirds(x)
    return jnp.concatenate([h, m, h], 1)


def dot(a, b, da, db):
    return lax.dot_general(
        a,
        b,
        (((da,), (db,)), ((), ())),
        precision=lax.Precision.HIGHEST,
        preferred_element_type=F32,
    )


def lanes(x, j):
    return jnp.broadcast_to(x[:, j : j + 1], x.shape)


def inverse128(a, steps_ref):
    n = a.shape[0] // 8
    sub = lax.broadcasted_iota(jnp.int32, (8, 128), 0)
    lane = lax.broadcasted_iota(jnp.int32, (8, 128), 1)
    count = [0]

    def keep(x):
        at = 8 * count[0]
        count[0] += 1
        steps_ref[at : at + 8, :] = x
        return at

    def row(at, r):
        return steps_ref[pl.ds(at + r, 8, stride=0), :]

    part = [a[8 * i : 8 * i + 8, :] for i in range(n)]
    column = [lanes(part[0], c) for c in range(8)]
    inverse = []
    for k in range(n):
        here = (lane >= 8 * k) & (lane < 8 * k + 8)
        kept = [keep(c) for c in column]
        pivot = {(r, s): row(kept[s], r) for s in range(8) for r in range(s, 8)}
        low, scale, solved = {}, [], []
        if k + 1 < n:
            below = [lanes(part[k + 1], 8 * k + s) for s in range(8)]
            column = [lanes(part[k + 1], 8 * k + 8 + c) for c in range(8)]
        for s in range(8):
            reciprocal = 1.0 / pivot[s, s]
            scale.append(lax.rsqrt(pivot[s, s]))
            for r in range(s + 1, 8):
                low[r, s] = pivot[r, s] * scale[s]
            for t in range(s + 1, 8):
                for r in range(t, 8):
                    pivot[r, t] = pivot[r, t] - (pivot[r, s] * pivot[t, s]) * reciprocal
            if k + 1 < n:
                x = below[s]
                for t in range(s):
                    x = x - low[s, t] * solved[t]
                x = x * scale[s]
                solved.append(x)
                at = keep(x)
                for c in range(8):
                    column[c] = column[c] - x * row(at, c)
        at = keep(jnp.where(here, jnp.where(lane == sub + 8 * k, 1.0, 0.0).astype(F32), part[k]))
        u = []
        for s in range(8):
            x = row(at, s)
            for t in range(s):
                x = x - low[s, t] * u[t]
            u.append(x * scale[s])
        x = u[7]
        for s in range(6, -1, -1):
            x = jnp.where(sub == s, u[s], x)
        inverse.append(jnp.where(lane <= sub + 8 * k, x, 0.0))
        if k + 1 < n:
            x = jnp.where(here, 0.0, part[k + 1])
            for s in range(8):
                x = x - solved[s] * u[s]
            part[k + 1] = x
        if k + 2 < n:
            for s in range(7, -1, -1):
                for t in range(s + 1, 8):
                    u[s] = u[s] - low[t, s] * u[t]
                u[s] = u[s] * scale[s]
            for i in range(k + 2, n):
                x = jnp.where(here, 0.0, part[i])
                for s in range(8):
                    x = x - lanes(part[i], 8 * k + s) * u[s]
                part[i] = x
    return jnp.concatenate(inverse, 0)


def inverse_factor(a_ref, out_ref, steps_ref):
    h = a_ref.shape[0] // 2
    inv0 = inverse128(a_ref[:h, :h], steps_ref)
    upper = dot(inv0, a_ref[:h, h:], 1, 0)
    inv1 = inverse128(a_ref[h:, h:] - dot(upper, upper, 0, 0), steps_ref)
    out_ref[:h, :h] = inv0
    out_ref[:h, h:] = jnp.zeros((h, h), F32)
    out_ref[h:, :h] = -dot(inv1, dot(upper, inv0, 0, 0), 1, 0)
    out_ref[h:, h:] = inv1


def first_kernel(place_ref, tile_ref, out_ref, steps_ref):
    root = (place_ref[0] == 0) & (place_ref[1] == 0)

    @pl.when(root)
    def _():
        inverse_factor(tile_ref, out_ref, steps_ref)

    @pl.when(jnp.logical_not(root))
    def _():
        out_ref[...] = tile_ref[...]


def solve(left, right, inv0, low, inv1):
    first = product(left6(left), inv0)
    return first, product(left6(right - product(left6(first), low)), inv1)


def second_kernel(place_ref, own_ref, other_ref, inv0_ref, low_ref, inv1_ref, tile_ref, steps_ref):
    first = place_ref[1] == 0
    inv0 = jnp.where(first, own_ref[0], other_ref[0])
    inv0_ref[...] = inv0
    low = product(left6(jnp.where(first, own_ref[1], other_ref[1])), right6(inv0))
    low_ref[...] = low
    corner = jnp.where(first, other_ref[0], own_ref[0])
    tile_ref[...] = corner - product(left6(low), right6(low))
    inverse_factor(tile_ref, inv1_ref, steps_ref)


def slot_of(place_ref, hop):
    flip = jnp.where(place_ref[1] == 0, hop, (hop % 2) * 2 + hop // 2)
    return jnp.bitwise_xor(lax.rem(place_ref[0], 8) // 2, flip)


def update(place_ref, keep_ref, tile, rows, panel, t, s):
    wanted = 2 * s + place_ref[1] <= t * place_ref[2] + place_ref[0]
    kept = jnp.where(keep_ref[t, s] == 1, tile, 0.0)
    return kept - jnp.where(wanted, product(rows, panel), 0.0)


def third_kernel(
    place_ref, keep_ref, inv0_ref, low_ref, inv1_ref, own_ref, other_ref, at_ref, a_ref, b_ref, tiles_ref,
    out_ref, rows_ref, hops, tiles, result, sems, hop_sems, out_sems,
):
    core0 = place_ref[1] == 0
    edge, count = tiles_ref.shape[-1], tiles_ref.shape[0]
    copy = pltpu.make_async_copy
    loads = [
        copy(ref, hops.at[i], hop_sems.at[i])
        for i, ref in enumerate((own_ref, other_ref, at_ref, a_ref, b_ref))
    ]
    loads.append(copy(tiles_ref, tiles, sems.at[0]))
    for load in loads:
        load.start()
    factors = right6(inv0_ref[...]), right6(low_ref[...]), right6(inv1_ref[...])
    row = lax.broadcasted_iota(jnp.int32, (edge, edge), 0)
    lower = row >= lax.broadcasted_iota(jnp.int32, (edge, edge), 1)
    for load in loads[:5]:
        load.wait()
    lefts = [jnp.where(core0, hops[0, t], hops[1, t]) for t in range(count)]
    rights = [jnp.where(core0, hops[1, t], hops[0, t]) for t in range(count)]
    for i in range(2, 5):
        lefts.append(jnp.where(core0, hops[i, 0], hops[i, 1]))
        rights.append(jnp.where(core0, hops[i, 1], hops[i, 0]))
    inv0, low, inv1 = factors
    firsts = [product(left6(x), inv0) for x in lefts]
    rests = [x - product(left6(first), low) for x, first in zip(rights, firsts)]
    seconds = [product(left6(x), inv1) for x in rests]
    stores, rows = [], []
    for t in range(count):
        i = t * place_ref[2] + place_ref[0]
        first, second = firsts[t], seconds[t]
        first = jnp.where((i > 0) | lower, first, 0.0)
        second = jnp.where((i > 1) | ((i == 1) & lower), second, 0.0)
        result[t, 3] = jnp.where(core0, first, second)
        rows_ref[t, :, :edge] = first
        rows_ref[t, :, edge:] = second
        rows.append(left3(jnp.concatenate([first, second], 1)))
        stores.append(copy(result.at[t, 3], out_ref.at[t, 0], out_sems.at[t, 3]))
    panels = [right3(jnp.concatenate(both, 1)) for both in zip(firsts[count:], seconds[count:])]
    loads[5].wait()
    for i in range(3):
        s = slot_of(place_ref, i)
        for t in range(count):
            result[t, i] = update(place_ref, keep_ref, tiles[t, s], rows[t], panels[i], t, s)
    for store in stores:
        store.start()
    for i in range(3):
        s = slot_of(place_ref, i)

        @pl.when(s > 0)
        def _():
            for t in range(count):
                copy(result.at[t, i], out_ref.at[t, s], out_sems.at[t, i]).start()
            for t in range(count):
                copy(result.at[t, i], out_ref.at[t, s], out_sems.at[t, i]).wait()

    for store in stores:
        store.wait()


def fourth_kernel(
    place_ref, keep_ref, inv0_ref, low_ref, inv1_ref, rows_ref, c_ref, tiles_ref, _,
    out_ref, tiles, result, sems, out_sems,
):
    s = slot_of(place_ref, 3)

    @pl.when(s > 0)
    def _():
        core0 = place_ref[1] == 0
        count = tiles.shape[0]
        copy = pltpu.make_async_copy
        loads = [copy(tiles_ref.at[t, s], tiles.at[t], sems.at[t]) for t in range(count)]
        stores = [copy(result.at[t], out_ref.at[t, s], out_sems.at[t]) for t in range(count)]
        for load in loads:
            load.start()
        factors = right6(inv0_ref[...]), right6(low_ref[...]), right6(inv1_ref[...])
        both = solve(jnp.where(core0, c_ref[0], c_ref[1]), jnp.where(core0, c_ref[1], c_ref[0]), *factors)
        panel = right3(jnp.concatenate(both, 1))
        rows = [left3(rows_ref[t]) for t in range(count)]
        for load in loads:
            load.wait()
        for t in range(count):
            result[t] = update(place_ref, keep_ref, tiles[t], rows[t], panel, t, s)
            stores[t].start()
        for store in stores:
            store.wait()


def call(kernel, name, outs, specs, scratch, flops, *args, out_specs=VMEM, aliases={}):
    return pl.pallas_call(
        kernel,
        out_shape=outs,
        in_specs=specs,
        out_specs=out_specs,
        input_output_aliases=aliases,
        scratch_shapes=scratch,
        name=name,
        cost_estimate=pl.CostEstimate(flops=flops, bytes_accessed=1 << 20, transcendentals=0),
        compiler_params=pltpu.CompilerParams(vmem_limit_bytes=48 << 20),
    )(*args)


def after(x, *earlier):
    return lax.optimization_barrier((x,) + earlier)[0]


def local(matrix, keep_mask):
    tiles = matrix[:, 0, :, 0]
    row_count, pair_count, edge = tiles.shape[0], tiles.shape[1], tiles.shape[-1]
    n = lax.axis_size("row")
    p, q = lax.axis_index("row"), lax.axis_index("col")
    tile_row = jnp.arange(row_count, dtype=jnp.int32)[:, None] * n + p
    tile_col = 2 * jnp.arange(pair_count, dtype=jnp.int32)[None, :] + q
    keep = (
        ((keep_mask[:, 0, :, 0] == 1) | (tile_row == tile_col))
        & (tile_row >= tile_col)
        & (tile_row - tile_col <= HALF_BAND)
    ).astype(jnp.int32)
    place = jnp.stack([p, q, jnp.int32(n)]).astype(jnp.int32)

    def send(x, pairs):
        return lax.ppermute(x, ("row", "col"), [(2 * a + b, 2 * c + d) for a, b, c, d in pairs])

    mine = jnp.where(keep[0, 0] == 1, matrix[0, 0, 0, 0], 0.0)
    high = []
    while 8 << len(high) < n:
        high.append(8 << len(high))
    sources = [i for i in range(n) if i % 8 > 1]
    flips = (2, 4)

    def chosen(ps):
        return sum([(p == i).astype(jnp.int32) for i in ps]) > 0

    source = [(0, 0), (1, 0), (1, 1)]
    tile = jax.ShapeDtypeStruct((edge, edge), F32)
    room = pltpu.VMEM((STEPS, edge // 2), F32)
    held = call(first_kernel, "first", tile, [SMEM, VMEM], [room], 10**9, place, mine)
    for bit in high[1:]:
        r = send(held, [(i, c, i + bit, c) for i, c in source])
        held = jnp.where(chosen([i + bit for i, _ in source]), r, held)
        source = source + [(i + bit, c) for i, c in source]
    steps = (2, high[0], high[0] + 2)
    received = [send(held, [(i, c, i + bit, c) for i, c in source]) for bit in steps]
    trail = mine
    for size in high:
        r = send(trail, [(i, c, i + size, c) for i in range(2, size) if i % 8 > 1 for c in range(2)])
        trail = jnp.where((p >= size) & (p < 2 * size), r, trail)
    for bit, r in zip(steps, received):
        held = jnp.where(chosen([i + bit for i, _ in source]), r, held)
    source = source + [(i + bit, c) for bit in steps for i, c in source]
    across = send(held, [(i, c, i ^ 1, c) for i, c in source])
    up = send(held, [(i, c, i + 4, c) for i, c in source])
    both = send(held, [(i, c, (i ^ 1) + 4, c) for i, c in source])
    below, even = jnp.bitwise_and(p, 4) == 0, jnp.bitwise_and(p, 1) == 0
    straight, crossed = jnp.where(below, held, up), jnp.where(below, across, both)
    row0 = jnp.where(even, straight, crossed)
    row1 = jnp.where(even, crossed, straight)
    lead = jnp.stack([jnp.where(q == 0, row0, row1), row1])

    r1 = send(
        trail,
        [(i, i % 2, i ^ 1, i % 2) for i in sources] + [(i, 1 - i % 2, i, i % 2) for i in sources],
    )
    r2 = send(trail, [(i, 1 - i % 2, i ^ 1, i % 2) for i in sources])
    lead_other = send(lead, [(i, c, i, 1 - c) for i in range(n) for c in range(2)])
    home = jnp.bitwise_and(p, 1) == q
    at = jnp.stack([jnp.where(home, trail, r1), jnp.where(home, r1, r2)])
    ra = send(at, [(i, c, i ^ flips[c], c) for i in range(n) for c in range(2)])
    rb = send(at, [(i, c, i ^ flips[1 - c], c) for i in range(n) for c in range(2)])

    lead, at = lax.optimization_barrier((lead, at))
    inv0, low, inv1 = call(
        second_kernel, "second", [tile, tile, tile], [SMEM, VMEM, VMEM],
        [pltpu.VMEM((edge, edge), F32), room], 10**10, place, lead, lead_other, out_specs=[VMEM] * 3,
    )
    rc = send(ra, [(i, c, i ^ flips[1 - c], c) for i in range(n) for c in range(2)])
    own = jnp.stack([mine, jnp.where(keep[1, 0] == 1, matrix[1, 0, 0, 0], 0.0)])
    other = send(after(own, inv1), [(i, c, i, 1 - c) for i in range(n) for c in range(2)])
    three, five = pltpu.SemaphoreType.DMA((3,)), pltpu.SemaphoreType.DMA((5,))
    out, rows = call(
        third_kernel, "third",
        [
            jax.ShapeDtypeStruct(tiles.shape, F32),
            jax.ShapeDtypeStruct((row_count, edge, 2 * edge), F32),
        ],
        [SMEM, SMEM] + [VMEM] * 3 + [ANY] * 6,
        [
            pltpu.VMEM((5,) + at.shape, F32),
            pltpu.VMEM(tiles.shape, F32),
            pltpu.VMEM((row_count, 4, edge, edge), F32),
            three,
            five,
            pltpu.SemaphoreType.DMA((row_count, 4)),
        ],
        10**10, place, keep, inv0, low, inv1, own, other, at, ra, rb, tiles, out_specs=[ANY, VMEM],
    )
    out = call(
        fourth_kernel, "fourth", jax.ShapeDtypeStruct(tiles.shape, F32),
        [SMEM, SMEM] + [VMEM] * 5 + [ANY] * 2,
        [pltpu.VMEM(own.shape, F32), pltpu.VMEM(own.shape, F32), three, three],
        10**10, place, keep, inv0, low, inv1, rows, rc, tiles, out, out_specs=ANY, aliases={8: 0},
    )
    return out[:, None, :, None]


def solution(mesh):
    return jax.shard_map(
        local,
        mesh=mesh,
        in_specs=(P(None, "row", None, "col", None, None), P(None, "row", None, "col")),
        out_specs=P(None, "row", None, "col", None, None),
        check_vma=False,
    )
```
